512 devices in a mesh: section: 16 (over z_hi, y, core), blk: 32 (over x, z_lo).
Axes of the slice: x: 4, y: 4, z: 16 (z_hi: 2, z_lo: 8; z = z_hi * 8 + z_lo), core: 2. Of those that a mesh axis runs over, the one named last changes fastest.
Arguments:
- acts: bfloat16 [16, 1024, 4096], P('section', 'blk'), may hold values from -3 to 3
- q_in: bfloat16 [16, 1024, 4096], P('section', 'blk'), may hold values from -24 to 24
- k_in: bfloat16 [16, 1024, 4096], P('section', 'blk'), may hold values from -24 to 24
- v_in: bfloat16 [16, 1024, 4096], P('section', 'blk'), may hold values from -6 to 6
- modulation: float32 [16, 40, 4096], P('section'), may hold values from -4.5 to 4.5
- q_gain: float32 [16, 4096], P('section'), may hold values from 0.8 to 5
- k_gain: float32 [16, 4096], P('section'), may hold values from 0.8 to 5
- patch_len: int32 [16], P('section'), may hold values from 512 to 1024, as said below
- timestep: int32 [1], replicated, may hold values from 0 to 39
Outputs:
- layer_out: bfloat16 [16, 1024, 4096], P('section', 'blk')
- passed: bfloat16 [16, 1024, 4096], P('section', 'blk')
The draws below stay inside these ranges and needn't reach their ends.
Inputs may be any that keep to these rules, and one draw needn't show every extreme that they name: `patch_len`: some section's micro-batch is full in every draw.
All inputs are finite; a program needn't handle non-finite values.
Results may differ from the reference program's by a relative error of at most 0.007.
The reference program's roundings to bfloat16 on the way (of `weights`) count: a program that leaves them out, or rounds other values in their place, can miss the bound.
Values may be sent and summed in bfloat16 or wider, within the bound.
A program may use at most 64 MiB of HBM per device.

```python
import math
import jax
import jax.numpy as jnp
from jax import lax

HEADS = 32
HEAD = 128
CHANNELS = 4096
STEPS = 40
PATCH = 1024
LAYERS = 16


def paired_fields(key):
    base_key = jax.random.fold_in(key, 101)
    shape = (LAYERS, PATCH, CHANNELS)
    queries = jax.random.normal(jax.random.fold_in(base_key, 1), shape, jnp.float32)
    key_rows = jax.random.normal(jax.random.fold_in(base_key, 2), shape, jnp.float32)
    return (jnp.clip(queries, -6.0, 6.0), jnp.clip(key_rows, -6.0, 6.0))


def draw_q_in(key, part):
    return paired_fields(key)[0].astype(jnp.bfloat16)


def draw_k_in(key, part):
    return paired_fields(key)[1].astype(jnp.bfloat16)


def gain_field(key, salt):
    base_key = jax.random.fold_in(key, salt)
    spread = jax.random.uniform(jax.random.fold_in(base_key, 1), (LAYERS, CHANNELS), jnp.float32, math.log(0.8), math.log(2.5))
    return jnp.exp(spread)


def draw_q_gain(key, part):
    return gain_field(key, 211)


def draw_k_gain(key, part):
    return gain_field(key, 307)


def draw_patch_len(key, part):
    base_key = jax.random.fold_in(key, 401)
    lengths = jax.random.randint(jax.random.fold_in(base_key, 1), (LAYERS,), PATCH // 2, PATCH + 1)
    chosen = jax.random.randint(jax.random.fold_in(base_key, 2), (), 0, LAYERS)
    return jnp.where(jnp.arange(LAYERS, dtype=jnp.int32) == chosen, PATCH, lengths).astype(jnp.int32)


def levels(stream_key, shape, pieces, least, high):
    gain, own = 1.0, jax.random.fold_in(stream_key, 6)
    for position, parts in pieces:
        draws = jnp.exp(jax.random.uniform(jax.random.fold_in(own, position), (parts,), jnp.float32, least / len(pieces), high / len(pieces)))
        gain = gain * jnp.repeat(draws, shape[position] // parts).reshape([-1 if axis == position else 1 for axis in range(len(shape))])
    return gain


def scatter_about(rng, dims, deviation, bound, split=(), held_as=jnp.bfloat16):
    level = levels(rng, dims, split, -0.22, 0.18) if split else 1.0
    result = jax.random.normal(rng, dims, jnp.float32) * deviation * level
    return jnp.minimum(jnp.maximum(result, -bound), bound).astype(held_as)


def setup_inputs(seed: int = 0) -> dict:
    keys = jax.random.split(jax.random.key(seed), 10)
    return {
        "acts": scatter_about(keys[0], (LAYERS, PATCH, CHANNELS), 0.5, 3.0, ((0, 16), (1, 32))),
        "q_in": draw_q_in(jax.random.fold_in(keys[9], 71), 0),
        "k_in": draw_k_in(jax.random.fold_in(keys[9], 71), 0),
        "v_in": scatter_about(keys[3], (LAYERS, PATCH, CHANNELS), 1.0, 6.0, ((0, 16), (1, 32))),
        "modulation": scatter_about(keys[4], (LAYERS, STEPS, CHANNELS), 1.5, 4.5, ((0, 16),), jnp.float32),
        "q_gain": draw_q_gain(jax.random.fold_in(keys[9], 71), 0),
        "k_gain": draw_k_gain(jax.random.fold_in(keys[9], 71), 0),
        "patch_len": draw_patch_len(jax.random.fold_in(keys[9], 71), 0),
        "timestep": jax.random.randint(keys[8], (1,), 0, STEPS).astype(jnp.int32),
    }


def unit_rows(block, gains):
    values = block.astype(jnp.float32)
    scaled = values * lax.rsqrt(lax.optimization_barrier(jnp.mean(values * values, axis=-1, keepdims=True)) + 1e-06)
    return (scaled * gains).astype(jnp.bfloat16)

def one_section(acts_rows, q_rows, k_rows, v_rows, table, q_row, k_row, length, step):
    gate = lax.dynamic_index_in_dim(table, step, 0, keepdims=False)
    queries = unit_rows(q_rows, q_row).reshape(PATCH, HEADS, HEAD)
    key_rows = unit_rows(k_rows, k_row).reshape(PATCH, HEADS, HEAD)
    values = v_rows.reshape(PATCH, HEADS, HEAD)
    usable = jnp.arange(PATCH, dtype=jnp.int32) < length
    score_scale = 1.0 / math.sqrt(HEAD)

    def per_head(operands):
        q_head, k_head, v_head = operands
        scores = jnp.dot(q_head, k_head.T, preferred_element_type=jnp.float32) * score_scale
        scores = jnp.where(usable[None, :], scores, -1e+30)
        peak = lax.optimization_barrier(jnp.max(scores, axis=-1, keepdims=True))
        weights = jnp.exp(scores - peak)
        total = lax.optimization_barrier(jnp.sum(weights, axis=-1, keepdims=True))
        return jnp.dot(weights.astype(jnp.bfloat16), v_head, preferred_element_type=jnp.float32) / total
    heads_out = lax.map(per_head, (jnp.transpose(queries, (1, 0, 2)), jnp.transpose(key_rows, (1, 0, 2)), jnp.transpose(values, (1, 0, 2))))
    attention = jnp.transpose(heads_out, (1, 0, 2)).reshape(PATCH, CHANNELS)
    return (acts_rows.astype(jnp.float32) + gate * attention).astype(jnp.bfloat16)

def reference(acts, q_in, k_in, v_in, modulation, q_gain, k_gain, patch_len, timestep):
    step = timestep[0]

    def per_section(operands):
        acts_rows, q_rows, k_rows, v_rows, table, q_row, k_row, length = operands
        return one_section(acts_rows, q_rows, k_rows, v_rows, table, q_row, k_row, length, step)
    layer_out = lax.map(per_section, (acts, q_in, k_in, v_in, modulation, q_gain, k_gain, patch_len))
    passed = jnp.roll(layer_out, 1, axis=0)
    return (layer_out, passed)
```

```python
import math

import jax
import jax.numpy as jnp
from jax import lax
from jax.sharding import PartitionSpec as P

HEAD = 128


def unit_rows(block, gains):
    values = block.astype(jnp.float32)
    scaled = values * lax.rsqrt(jnp.mean(values * values, axis=-1, keepdims=True) + 1e-06)
    return (scaled * gains).astype(jnp.bfloat16)


def body(acts, q_in, k_in, v_in, modulation, q_gain, k_gain, patch_len, timestep):
    gate = lax.dynamic_index_in_dim(modulation[0], timestep[0], 0, keepdims=False)
    rows, channels = acts.shape[1:]
    heads = channels // HEAD
    queries = unit_rows(q_in[0], q_gain[0])
    keys = unit_rows(k_in[0], k_gain[0])
    packed = jnp.stack([queries, keys, v_in[0]]).reshape(3, rows, heads, HEAD)
    packed = jnp.transpose(packed, (2, 0, 1, 3))
    owned = lax.all_to_all(packed, "blk", 0, 0, tiled=True)
    owned = jnp.transpose(owned, (1, 0, 2, 3)).reshape(3, heads * rows, HEAD)
    scores = jnp.dot(owned[0], owned[1].T, preferred_element_type=jnp.float32) * (1.0 / math.sqrt(HEAD))
    usable = jnp.arange(heads * rows, dtype=jnp.int32) < patch_len[0]
    scores = jnp.where(usable[None, :], scores, -1e30)
    weights = jnp.exp(scores - jnp.max(scores, axis=-1, keepdims=True))
    total = jnp.sum(weights, axis=-1, keepdims=True)
    mixed = jnp.dot(weights.astype(jnp.bfloat16), owned[2], preferred_element_type=jnp.float32) / total
    mixed = mixed.astype(jnp.bfloat16).reshape(heads, rows, HEAD)
    back = lax.all_to_all(mixed, "blk", 0, 0, tiled=True)
    attention = jnp.transpose(back, (1, 0, 2)).reshape(rows, channels).astype(jnp.float32)
    layer_out = (acts[0].astype(jnp.float32) + gate * attention).astype(jnp.bfloat16)
    sections = lax.axis_size("section")
    passed = lax.ppermute(layer_out, "section", [(i, (i + 1) % sections) for i in range(sections)])
    return (layer_out[None], passed[None])


def solution(mesh):
    return jax.shard_map(
        body,
        mesh=mesh,
        in_specs=(
            P("section", "blk", None),
            P("section", "blk", None),
            P("section", "blk", None),
            P("section", "blk", None),
            P("section", None, None),
            P("section", None),
            P("section", None),
            P("section"),
            P(),
        ),
        out_specs=(P("section", "blk", None), P("section", "blk", None)),
        check_vma=False,
    )
```

```python
import functools
import math

import jax
import jax.numpy as jnp
from jax import lax
from jax.experimental import pallas as pl
from jax.experimental.pallas import tpu as pltpu
from jax.sharding import PartitionSpec as P

HEAD = 128
GROUP = 4
LAG = 3
MESH = pl.DeviceIdType.MESH


def xor(a, b, bits):
    return sum((((a // 2**i) + (b // 2**i)) % 2) * 2**i for i in range(bits))


def kernel(
    n, sections,
    acts_hbm, q_hbm, k_hbm, v_hbm, mod_hbm, q_gain, k_gain, length_ref, step_ref,
    out_hbm, pass_hbm,
    acts, q_raw, k_raw, v_raw, table, q_unit, k_unit, keys, values, queries, mixed, attention, layer_out,
    load_sem, v_send, k_send, q_send, o_send, v_recv, k_recv, q_recv, o_recv, pass_send, pass_recv, out_sem,
):
    bits = n.bit_length() - 1
    groups = n // GROUP
    rows = acts.shape[0]
    span = GROUP * HEAD
    me = lax.axis_index("blk")
    sec = lax.axis_index("section")
    after = (sec + 1) % sections
    before = (sec + sections - 1) % sections

    barrier = pltpu.get_barrier_semaphore()

    def greet(t, c):
        pl.semaphore_signal(barrier, inc=1, device_id={"section": sec, "blk": xor(me, t, bits)}, device_id_type=MESH)
        return c

    lax.fori_loop(1, n, greet, 0)
    pl.semaphore_signal(barrier, inc=1, device_id={"section": before, "blk": me}, device_id_type=MESH)

    loads = [
        pltpu.make_async_copy(src.at[0], dst, load_sem.at[i])
        for i, (src, dst) in enumerate(
            ((k_hbm, k_raw), (v_hbm, v_raw), (q_hbm, q_raw), (acts_hbm, acts), (mod_hbm, table))
        )
    ]
    for load in loads:
        load.start()

    def unit(raw, gain, out):
        block = raw[...].astype(jnp.float32)
        scaled = block * lax.rsqrt(jnp.mean(block * block, axis=-1, keepdims=True) + 1e-06)
        out[...] = (scaled * gain[...]).astype(jnp.bfloat16)

    def lanes(head):
        return pl.ds(pl.multiple_of(head * HEAD, HEAD), HEAD)

    def token_rows(block):
        return pl.ds(pl.multiple_of(block * rows, rows), rows)

    mine = token_rows(me)

    def send(src, dst, send_sem, recv_sem, partner):
        pltpu.make_async_remote_copy(
            src_ref=src, dst_ref=dst, send_sem=send_sem, recv_sem=recv_sem,
            device_id={"section": sec, "blk": partner}, device_id_type=MESH,
        ).start()

    def await_bytes(ref, sem):
        pltpu.make_async_copy(ref, ref, sem).wait()

    loads[0].wait()
    unit(k_raw, k_gain, k_unit)
    loads[1].wait()
    pl.semaphore_wait(barrier, n)

    def send_v(t, c):
        partner = xor(me, t, bits)
        send(v_raw.at[:, lanes(partner)], values.at[mine], v_send, v_recv, partner)
        return c

    def send_k(t, c):
        partner = xor(me, t, bits)
        send(k_unit.at[:, lanes(partner)], keys.at[mine], k_send, k_recv, partner)
        return c

    def send_q(t, c):
        partner = xor(me, t, bits)
        send(q_unit.at[:, lanes(partner)], queries.at[token_rows(t)], q_send, q_recv.at[t // GROUP], partner)
        return c

    lax.fori_loop(1, n, send_v, 0)
    lax.fori_loop(1, n, send_k, 0)
    loads[2].wait()
    unit(q_raw, q_gain, q_unit)
    lax.fori_loop(1, n, send_q, 0)
    values[mine] = v_raw[:, lanes(me)]
    keys[mine] = k_unit[:, lanes(me)]
    queries[pl.ds(0, rows)] = q_unit[:, lanes(me)]

    others = pl.ds(0, (n - 1) * rows)
    place = lax.broadcasted_iota(jnp.int32, (1, n * rows), 1)
    bias = jnp.where(place < length_ref[0], 0.0, -1e30)
    scale = math.log2(math.e) / math.sqrt(HEAD)
    await_bytes(values.at[others], v_recv)
    await_bytes(keys.at[others], k_recv)

    def attend(g):
        here = pl.ds(pl.multiple_of(g * GROUP * rows, GROUP * rows), GROUP * rows)
        scores = lax.dot_general(
            queries[here], keys[...], (((1,), (1,)), ((), ())), preferred_element_type=jnp.float32
        )
        scores = scores * scale + bias
        weights = jnp.exp2(scores - jnp.max(scores, axis=-1, keepdims=True))
        total = jnp.sum(weights, axis=-1, keepdims=True)
        product = jnp.dot(weights.astype(jnp.bfloat16), values[...], preferred_element_type=jnp.float32)
        mixed[here] = (product / total).astype(jnp.bfloat16)

    def give_back(t, g):
        partner = xor(me, t, bits)
        send(mixed.at[token_rows(t)], attention.at[:, lanes(me)], o_send, o_recv.at[g], partner)

    loads[3].wait()
    loads[4].wait()
    step = step_ref[0]

    def pass_copy(slab, g):
        return pltpu.make_async_remote_copy(
            src_ref=layer_out.at[:, slab], dst_ref=pass_hbm.at[0, :, slab],
            send_sem=pass_send.at[g], recv_sem=pass_recv.at[g],
            device_id={"section": after, "blk": me}, device_id_type=MESH,
        )

    def own_copy(slab, g):
        return pltpu.make_async_copy(layer_out.at[:, slab], out_hbm.at[0, :, slab], out_sem.at[g])

    def slab_of(g):
        return pl.ds(pl.multiple_of(xor(me // GROUP, g, bits - 2) * span, span), span)

    def finish(g, count):
        await_bytes(mixed.at[pl.ds(0, count * rows)], o_recv.at[g])
        slab = slab_of(g)
        gate = table[pl.ds(step, 1), slab]
        mix = attention[:, slab].astype(jnp.float32)
        layer_out[:, slab] = (acts[:, slab].astype(jnp.float32) + gate * mix).astype(jnp.bfloat16)
        pass_copy(slab, g).start()
        own_copy(slab, g).start()

    def first_group():
        await_bytes(queries.at[pl.ds(0, (GROUP - 1) * rows)], q_recv.at[0])
        attend(0)
        for t in range(1, GROUP):
            give_back(t, 0)
        attention[:, lanes(me)] = mixed[pl.ds(0, rows)]

    def next_group(g):
        await_bytes(queries.at[pl.ds(0, GROUP * rows)], q_recv.at[g])
        attend(g)
        for t in range(GROUP):
            give_back(g * GROUP + t, g)

    lag = min(LAG, groups - 1)
    first_group()

    def early(g, c):
        next_group(g)
        return c

    lax.fori_loop(1, lag, early, 0)
    next_group(lag)
    finish(0, GROUP - 1)

    def both(g, c):
        next_group(g)
        finish(g - lag, GROUP)
        return c

    lax.fori_loop(lag + 1, groups, both, 0)

    def late(g, c):
        finish(g, GROUP)
        return c

    lax.fori_loop(groups - lag, groups, late, 0)

    await_bytes(values.at[others], v_send)
    await_bytes(values.at[others], k_send)
    await_bytes(values.at[others], q_send)
    await_bytes(values.at[others], o_send)

    def settle(g, c):
        slab = slab_of(g)
        own_copy(slab, g).wait()
        pass_copy(slab, g).wait()
        return c

    lax.fori_loop(0, groups, settle, 0)


def body(acts, q_in, k_in, v_in, modulation, q_gain, k_gain, patch_len, timestep):
    n = lax.axis_size("blk")
    sections = lax.axis_size("section")
    _, rows, channels = acts.shape
    groups = n // GROUP
    whole = pltpu.VMEM((rows, channels), jnp.bfloat16)
    owned = pltpu.VMEM((n * rows, HEAD), jnp.bfloat16)
    out = jax.ShapeDtypeStruct(acts.shape, jnp.bfloat16)
    dma = pltpu.SemaphoreType.DMA
    return pl.pallas_call(
        functools.partial(kernel, n, sections),
        out_shape=(out, out),
        in_specs=[pl.BlockSpec(memory_space=pl.ANY)] * 5
        + [pl.BlockSpec(memory_space=pltpu.VMEM)] * 2
        + [pl.BlockSpec(memory_space=pltpu.SMEM)] * 2,
        out_specs=[pl.BlockSpec(memory_space=pl.ANY)] * 2,
        scratch_shapes=[
            whole, whole, whole, whole,
            pltpu.VMEM(modulation.shape[1:], jnp.float32),
            whole, whole, owned, owned, owned, owned, whole, whole,
            dma((5,)), dma, dma, dma, dma, dma, dma,
            dma((groups,)), dma((groups,)), dma((groups,)), dma((groups,)), dma((groups,)),
        ],
        compiler_params=pltpu.CompilerParams(
            collective_id=0, has_side_effects=True, vmem_limit_bytes=60 << 20
        ),
        name="relay_attention",
    )(acts, q_in, k_in, v_in, modulation, q_gain, k_gain, patch_len, timestep)


def solution(mesh):
    return jax.shard_map(
        body,
        mesh=mesh,
        in_specs=(
            P("section", "blk", None),
            P("section", "blk", None),
            P("section", "blk", None),
            P("section", "blk", None),
            P("section", None, None),
            P("section", None),
            P("section", None),
            P("section"),
            P(),
        ),
        out_specs=(P("section", "blk", None), P("section", "blk", None)),
        check_vma=False,
    )
```

```python
import functools
import math

import jax
import jax.numpy as jnp
from jax import lax
from jax.experimental import pallas as pl
from jax.experimental.pallas import tpu as pltpu
from jax.sharding import PartitionSpec as P

HEAD = 128
GROUP = 4
LAG = 3
DEFER = 2
MESH = pl.DeviceIdType.MESH


def xor(a, b, bits):
    return sum((((a // 2**i) + (b // 2**i)) % 2) * 2**i for i in range(bits))


def kernel(
    n, sections,
    acts_hbm, q_hbm, k_hbm, v_hbm, mod_hbm, q_gain_hbm, k_gain_hbm, length_hbm, step_hbm,
    out_hbm, pass_hbm,
    acts, q_raw, k_raw, v_raw, table, q_gain, k_gain, length_ref, step_ref, q_unit, k_unit, keys, values, queries, mixed, attention, layer_out,
    load_sem, v_send, k_send, q_send, o_send, v_recv, k_recv, q_recv, o_recv, pass_send, pass_recv, out_sem, hop_buf, hop_send, hop_recv, go, turn,
):
    bits = n.bit_length() - 1
    groups = n // GROUP
    rows = acts.shape[0]
    span = GROUP * HEAD
    me = lax.axis_index("blk")
    sec = lax.axis_index("section")
    after = (sec + 1) % sections
    before = (sec + sections - 1) % sections

    barrier = pltpu.get_barrier_semaphore()

    def greet(t, c):
        pl.semaphore_signal(barrier, inc=1, device_id={"section": sec, "blk": xor(me, t, bits)}, device_id_type=MESH)
        return c

    def signal(sem, section):
        pl.semaphore_signal(sem, inc=1, device_id={"section": section, "blk": me}, device_id_type=MESH)

    half = sections // 2
    part = sec // half
    route = sec % half
    far = route == half - 1
    goal = (part + 1) % 2 * half
    odd = sec % 2

    lax.fori_loop(1, n, greet, 0)

    @pl.when(odd == 0)
    def _():
        signal(barrier, after)

    @pl.when(route > 0)
    def _():
        signal(barrier, before)

    @pl.when(route < half - 1)
    def _():
        signal(barrier, part * half + half - 1)

    @pl.when(part == 0)
    def _():
        signal(barrier, goal)

    @pl.when(sec == 0)
    def _():
        def call(r, c):
            signal(barrier, half + r)
            return c

        lax.fori_loop(0, half, call, 0)

    expected = n - 1 + odd + part
    expected += jnp.where(far, half - 1, 1)
    expected += jnp.where(sec == half, half, 0)

    loads = [
        pltpu.make_async_copy(src.at[0], dst, load_sem.at[i])
        for i, (src, dst) in enumerate(
            ((v_hbm, v_raw), (k_hbm, k_raw), (q_hbm, q_raw), (acts_hbm, acts), (mod_hbm, table))
        )
    ]
    loads += [
        pltpu.make_async_copy(src, dst, load_sem.at[5 + i])
        for i, (src, dst) in enumerate(
            ((k_gain_hbm, k_gain), (q_gain_hbm, q_gain), (length_hbm, length_ref), (step_hbm, step_ref))
        )
    ]
    for load in loads:
        load.start()

    def unit(raw, gain, out):
        block = raw[...].astype(jnp.float32)
        scaled = block * lax.rsqrt(jnp.mean(block * block, axis=-1, keepdims=True) + 1e-06)
        out[...] = (scaled * gain[...]).astype(jnp.bfloat16)

    def lanes(head):
        return pl.ds(pl.multiple_of(head * HEAD, HEAD), HEAD)

    def token_rows(block):
        return pl.ds(pl.multiple_of(block * rows, rows), rows)

    mine = token_rows(me)

    def send(src, dst, send_sem, recv_sem, partner):
        pltpu.make_async_remote_copy(
            src_ref=src, dst_ref=dst, send_sem=send_sem, recv_sem=recv_sem,
            device_id={"section": sec, "blk": partner}, device_id_type=MESH,
        ).start()

    def await_bytes(ref, sem):
        pltpu.make_async_copy(ref, ref, sem).wait()

    loads[0].wait()
    pl.semaphore_wait(barrier, expected)

    @pl.when(sec == half)
    def _():
        def call(r, c):
            signal(go, r)
            return c

        lax.fori_loop(0, half, call, 0)

    @pl.when(sec == sections - 2)
    def _():
        pl.semaphore_wait(turn, 1)

    def send_v(t, c):
        partner = xor(me, t, bits)
        send(v_raw.at[:, lanes(partner)], values.at[mine], v_send, v_recv, partner)
        return c

    def send_k(t, c):
        partner = xor(me, t, bits)
        send(k_unit.at[:, lanes(partner)], keys.at[mine], k_send, k_recv, partner)
        return c

    def send_q(t, c):
        partner = xor(me, t, bits)
        send(q_unit.at[:, lanes(partner)], queries.at[token_rows(t)], q_send, q_recv.at[t // GROUP], partner)
        return c

    lax.fori_loop(1, n, send_v, 0)
    loads[1].wait()
    loads[5].wait()
    unit(k_raw, k_gain, k_unit)
    lax.fori_loop(1, n, send_k, 0)
    loads[2].wait()
    loads[6].wait()
    unit(q_raw, q_gain, q_unit)
    lax.fori_loop(1, n, send_q, 0)
    values[mine] = v_raw[:, lanes(me)]
    keys[mine] = k_unit[:, lanes(me)]
    queries[pl.ds(0, rows)] = q_unit[:, lanes(me)]

    others = pl.ds(0, (n - 1) * rows)
    place = lax.broadcasted_iota(jnp.int32, (1, n * rows), 1)
    loads[7].wait()
    bias = jnp.where(place < length_ref[0], 0.0, -1e30)
    scale = math.log2(math.e) / math.sqrt(HEAD)
    await_bytes(values.at[others], v_send)
    await_bytes(values.at[others], k_send)
    await_bytes(values.at[others], q_send)

    @pl.when(sec == sections - 1)
    def _():
        signal(turn, before)

    def slab_of(g):
        return pl.ds(pl.multiple_of(xor(me // GROUP, g, groups.bit_length() - 1) * span, span), span)

    def pass_copy(slab, g, section):
        return pltpu.make_async_remote_copy(
            src_ref=layer_out.at[:, slab], dst_ref=pass_hbm.at[0, :, slab],
            send_sem=pass_send.at[g], recv_sem=pass_recv.at[g],
            device_id={"section": section, "blk": me}, device_id_type=MESH,
        )

    def hop_copy(slab, g, section):
        return pltpu.make_async_remote_copy(
            src_ref=layer_out.at[:, slab], dst_ref=hop_buf,
            send_sem=pass_send.at[g], recv_sem=hop_recv,
            device_id={"section": section, "blk": me}, device_id_type=MESH,
        )

    def relay(slab, g):
        return pltpu.make_async_remote_copy(
            src_ref=hop_buf, dst_ref=pass_hbm.at[0, :, slab],
            send_sem=hop_send, recv_sem=pass_recv.at[g],
            device_id={"section": goal, "blk": me}, device_id_type=MESH,
        )

    def hand_on():
        await_bytes(hop_buf, hop_recv)
        relay(slab_of(route), route).start()

    def hand_on_after(g):
        @pl.when((part == 0) & (route < half - 1) & (g == jnp.minimum(route + DEFER, groups - 1)))
        def _():
            hand_on()

    @pl.when((part == 1) & (route < half - 1))
    def _():
        hand_on()

    await_bytes(values.at[others], v_recv)
    await_bytes(keys.at[others], k_recv)

    def attend(g):
        here = pl.ds(pl.multiple_of(g * GROUP * rows, GROUP * rows), GROUP * rows)
        scores = lax.dot_general(
            queries[here], keys[...], (((1,), (1,)), ((), ())), preferred_element_type=jnp.float32
        )
        scores = scores * scale + bias
        weights = jnp.exp2(scores - jnp.max(scores, axis=-1, keepdims=True))
        total = jnp.sum(weights, axis=-1, keepdims=True)
        product = jnp.dot(weights.astype(jnp.bfloat16), values[...], preferred_element_type=jnp.float32)
        mixed[here] = (product / total).astype(jnp.bfloat16)

    def give_back(t, g):
        partner = xor(me, t, bits)
        send(mixed.at[token_rows(t)], attention.at[:, lanes(me)], o_send, o_recv.at[g], partner)

    loads[3].wait()
    loads[4].wait()
    loads[8].wait()
    step = step_ref[0]

    def own_copy(slab, g):
        return pltpu.make_async_copy(layer_out.at[:, slab], out_hbm.at[0, :, slab], out_sem.at[g])

    def finish(g, count):
        await_bytes(mixed.at[pl.ds(0, count * rows)], o_recv.at[g])
        slab = slab_of(g)
        gate = table[pl.ds(step, 1), slab]
        mix = attention[:, slab].astype(jnp.float32)
        layer_out[:, slab] = (acts[:, slab].astype(jnp.float32) + gate * mix).astype(jnp.bfloat16)
        direct = (route < half - 1) | (g == half - 1)

        @pl.when(direct)
        def _():
            pass_copy(slab, g, after).start()

        @pl.when(jnp.logical_not(direct))
        def _():
            hop_copy(slab, g, part * half + g).start()

        own_copy(slab, g).start()
        hand_on_after(g)

    def first_group():
        await_bytes(queries.at[pl.ds(0, (GROUP - 1) * rows)], q_recv.at[0])
        attend(0)
        for t in range(1, GROUP):
            give_back(t, 0)
        attention[:, lanes(me)] = mixed[pl.ds(0, rows)]

    def next_group(g):
        await_bytes(queries.at[pl.ds(0, GROUP * rows)], q_recv.at[g])
        attend(g)
        for t in range(GROUP):
            give_back(g * GROUP + t, g)

    lag = min(LAG, groups - 1)
    first_group()

    @pl.when(part == 0)
    def _():
        pl.semaphore_wait(go, 1)

    def early(g, c):
        next_group(g)
        return c

    lax.fori_loop(1, lag, early, 0)
    next_group(lag)
    finish(0, GROUP - 1)

    def both(g, c):
        next_group(g)
        finish(g - lag, GROUP)
        return c

    lax.fori_loop(lag + 1, groups, both, 0)

    def late(g, c):
        finish(g, GROUP)
        return c

    lax.fori_loop(groups - lag, groups, late, 0)

    await_bytes(values.at[others], o_send)

    @pl.when(route < half - 1)
    def _():
        await_bytes(hop_buf, hop_send)

    def settle(g, c):
        slab = slab_of(g)
        own_copy(slab, g).wait()
        pass_copy(slab, g, after).wait()
        return c

    lax.fori_loop(0, groups, settle, 0)


def body(acts, q_in, k_in, v_in, modulation, q_gain, k_gain, patch_len, timestep):
    n = lax.axis_size("blk")
    sections = lax.axis_size("section")
    _, rows, channels = acts.shape
    groups = n // GROUP
    whole = pltpu.VMEM((rows, channels), jnp.bfloat16)
    owned = pltpu.VMEM((n * rows, HEAD), jnp.bfloat16)
    out = jax.ShapeDtypeStruct(acts.shape, jnp.bfloat16)
    dma = pltpu.SemaphoreType.DMA
    return pl.pallas_call(
        functools.partial(kernel, n, sections),
        out_shape=(out, out),
        in_specs=[pl.BlockSpec(memory_space=pltpu.MemorySpace.HBM)] * 9,
        out_specs=[pl.BlockSpec(memory_space=pl.ANY)] * 2,
        scratch_shapes=[
            whole, whole, whole, whole,
            pltpu.VMEM(modulation.shape[1:], jnp.float32),
            pltpu.VMEM((1, channels), jnp.float32),
            pltpu.VMEM((1, channels), jnp.float32),
            pltpu.SMEM((1,), jnp.int32),
            pltpu.SMEM((1,), jnp.int32),
            whole, whole, owned, owned, owned, owned, whole, whole,
            dma((9,)), dma, dma, dma, dma, dma, dma,
            dma((groups,)), dma((groups,)), dma((groups,)), dma((groups,)), dma((groups,)),
            pltpu.VMEM((rows, GROUP * HEAD), jnp.bfloat16), dma, dma,
            pltpu.SemaphoreType.REGULAR, pltpu.SemaphoreType.REGULAR,
        ],
        compiler_params=pltpu.CompilerParams(
            collective_id=0, has_side_effects=True, vmem_limit_bytes=60 << 20
        ),
        name="relay_attention",
    )(acts, q_in, k_in, v_in, modulation, q_gain, k_gain, patch_len, timestep)


def solution(mesh):
    return jax.shard_map(
        body,
        mesh=mesh,
        in_specs=(
            P("section", "blk", None),
            P("section", "blk", None),
            P("section", "blk", None),
            P("section", "blk", None),
            P("section", None, None),
            P("section", None),
            P("section", None),
            P("section"),
            P(),
        ),
        out_specs=(P("section", "blk", None), P("section", "blk", None)),
        check_vma=False,
    )
```

```python
import functools
import math

import jax
import jax.numpy as jnp
from jax import lax
from jax.experimental import pallas as pl
from jax.experimental.pallas import tpu as pltpu
from jax.sharding import PartitionSpec as P

HEAD = 128
GROUP = 4
RUN = 8
LAG = 8
WAIT = 8
DEFER = 2
QWAIT = 0
INNER = 8
MESH = pl.DeviceIdType.MESH


def xor(a, b, bits):
    return sum((((a // 2**i) + (b // 2**i)) % 2) * 2**i for i in range(bits))


def kernel(
    n, sections,
    acts_hbm, q_hbm, k_hbm, v_hbm, mod_hbm, q_gain_hbm, k_gain_hbm, length_hbm, step_hbm,
    out_hbm, pass_hbm,
    acts, q_raw, k_raw, v_raw, table, q_gain, k_gain, length_ref, step_ref, q_unit, k_unit, keys, values, queries, mixed, attention, layer_out,
    load_sem, v_send, k_send, q_send, o_send, v_recv, k_recv, q_recv, o_recv, pass_send, pass_recv, out_sem, hop_near, hop_side, hop_send, hop_recv, go, turn,
):
    bits = n.bit_length() - 1
    groups = n // GROUP
    rows = acts.shape[0]
    span = GROUP * HEAD
    me = lax.axis_index("blk")
    sec = lax.axis_index("section")
    after = (sec + 1) % sections
    before = (sec + sections - 1) % sections

    barrier = pltpu.get_barrier_semaphore()

    flip = [(1 - 2 * ((me // 2**i) % 2)) * 2**i for i in range(bits)]
    inner = min(INNER, n)
    low = inner.bit_length() - 1
    low_group = GROUP.bit_length() - 1

    def flipped(base, first, count, which):
        for i in range(count):
            base = base + flip[first + i] * ((which // 2**i) % 2)
        return base

    def partner_in(base, j):
        return sum((flip[i] for i in range(low) if j >> i & 1), base)

    def each_partner(deliver):
        def block(hi, c):
            base = flipped(me, low, bits - low, hi)
            for j in sorted(range(inner), key=lambda j: (j % (inner // 2), j)):
                if j == 0:

                    @pl.when(hi > 0)
                    def _():
                        deliver(hi * inner, base)
                else:
                    deliver(hi * inner + j, partner_in(base, j))
            return c

        lax.fori_loop(0, n // inner, block, 0)

    def greet(t, partner):
        pl.semaphore_signal(barrier, inc=1, device_id={"section": sec, "blk": partner}, device_id_type=MESH)

    def signal(sem, section, blk):
        pl.semaphore_signal(sem, inc=1, device_id={"section": section, "blk": blk}, device_id_type=MESH)

    half = sections // 2
    part = sec // half
    route = sec % half
    far = route == half - 1
    helper = route < half - 1
    goal = (part + 1) % 2 * half
    source = part * half + half - 1
    odd = sec % 2
    run = min(RUN, n)
    spot = me % run

    def turned(place, side):
        late = (place >= run // 2) & (place < run)
        return late & (side == 0)

    def relay_blk(side):
        return me - jnp.where(turned(spot, side), 1, 0)

    near = jnp.logical_not(turned(spot, part))
    beside = turned(spot + 1, part)
    served = jnp.where(near, 1, 0) + jnp.where(beside, 1, 0)

    loads = [
        pltpu.make_async_copy(src.at[0], dst, load_sem.at[i])
        for i, (src, dst) in enumerate(
            ((v_hbm, v_raw), (k_hbm, k_raw), (q_hbm, q_raw), (acts_hbm, acts), (mod_hbm, table))
        )
    ]
    loads += [
        pltpu.make_async_copy(src, dst, load_sem.at[5 + i])
        for i, (src, dst) in enumerate(
            ((k_gain_hbm, k_gain), (q_gain_hbm, q_gain), (length_hbm, length_ref), (step_hbm, step_ref))
        )
    ]
    loads[0].start()
    each_partner(greet)
    for load in loads[1:]:
        load.start()

    @pl.when(odd == 0)
    def _():
        signal(barrier, after, me)

    @pl.when(route > 0)
    def _():
        signal(barrier, before, me)

    @pl.when(helper & near)
    def _():
        signal(barrier, source, me)

    @pl.when(helper & beside)
    def _():
        signal(barrier, source, me + 1)

    @pl.when((part == 0) & (near | far))
    def _():
        signal(barrier, goal, me)

    @pl.when((part == 0) & helper & beside)
    def _():
        signal(barrier, goal, me + 1)

    @pl.when(sec == 0)
    def _():
        def call(r, c):
            signal(barrier, half + r, relay_blk(1))
            return c

        lax.fori_loop(0, half - 1, call, 0)
        signal(barrier, sections - 1, me)

    expected = n - 1 + odd
    expected += jnp.where(far, half - 1, 1)
    expected += jnp.where(part == 1, jnp.where(far, 1, served), 0)
    expected += jnp.where(sec == half, half, 0)

    def unit(raw, gain, out):
        block = raw[...].astype(jnp.float32)
        scaled = block * lax.rsqrt(jnp.mean(block * block, axis=-1, keepdims=True) + 1e-06)
        out[...] = (scaled * gain[...]).astype(jnp.bfloat16)

    def lanes(head):
        return pl.ds(pl.multiple_of(head * HEAD, HEAD), HEAD)

    def token_rows(block):
        return pl.ds(pl.multiple_of(block * rows, rows), rows)

    mine = token_rows(me)

    def send(src, dst, send_sem, recv_sem, partner):
        pltpu.make_async_remote_copy(
            src_ref=src, dst_ref=dst, send_sem=send_sem, recv_sem=recv_sem,
            device_id={"section": sec, "blk": partner}, device_id_type=MESH,
        ).start()

    def await_bytes(ref, sem):
        pltpu.make_async_copy(ref, ref, sem).wait()

    loads[0].wait()
    pl.semaphore_wait(barrier, expected)

    @pl.when(sec == half)
    def _():
        def call(r, c):
            signal(go, r, relay_blk(0))
            return c

        lax.fori_loop(0, half - 1, call, 0)
        signal(go, half - 1, me)

    @pl.when(sec == sections - 2)
    def _():
        pl.semaphore_wait(turn, 1)

    def send_v(t, partner):
        send(v_raw.at[:, lanes(partner)], values.at[mine], v_send, v_recv, partner)

    def send_k(t, partner):
        send(k_unit.at[:, lanes(partner)], keys.at[mine], k_send, k_recv, partner)

    def send_q(t, partner):
        send(q_unit.at[:, lanes(partner)], queries.at[token_rows(t)], q_send, q_recv.at[t // GROUP], partner)

    def own(src, dst, sem):
        pltpu.make_async_copy(src, dst, sem).start()

    each_partner(send_v)
    loads[1].wait()
    loads[5].wait()
    unit(k_raw, k_gain, k_unit)
    each_partner(send_k)
    loads[2].wait()
    loads[6].wait()
    unit(q_raw, q_gain, q_unit)
    others = pl.ds(0, (n - 1) * rows)
    if QWAIT > 0:
        await_bytes(values.at[others], v_send)
    if QWAIT > 1:
        await_bytes(values.at[others], k_send)
    each_partner(send_q)
    own(v_raw.at[:, lanes(me)], values.at[mine], v_recv)
    own(k_unit.at[:, lanes(me)], keys.at[mine], k_recv)
    own(q_unit.at[:, lanes(me)], queries.at[pl.ds(0, rows)], q_recv.at[0])

    place = lax.broadcasted_iota(jnp.int32, (1, n * rows), 1)
    loads[7].wait()
    bias = jnp.where(place < length_ref[0], 0.0, -1e30)
    scale = math.log2(math.e) / math.sqrt(HEAD)
    @pl.when(sec == sections - 1)
    def _():
        if QWAIT < 1:
            await_bytes(values.at[others], v_send)
        if QWAIT < 2:
            await_bytes(values.at[others], k_send)
        await_bytes(values.at[others], q_send)
        signal(turn, before, me)

    def slab_base(g):
        return flipped(me, low_group, bits - low_group, g)

    def slab_of(g):
        return pl.ds(pl.multiple_of(slab_base(g) // GROUP * span, span), span)

    def pass_copy(slab, g, section):
        return pltpu.make_async_remote_copy(
            src_ref=layer_out.at[:, slab], dst_ref=pass_hbm.at[0, :, slab],
            send_sem=pass_send.at[g], recv_sem=pass_recv.at[g],
            device_id={"section": section, "blk": me}, device_id_type=MESH,
        )

    def hop_copy(slab, g, buf, lane, blk):
        return pltpu.make_async_remote_copy(
            src_ref=layer_out.at[:, slab], dst_ref=buf,
            send_sem=pass_send.at[g], recv_sem=hop_recv.at[lane],
            device_id={"section": part * half + g, "blk": blk}, device_id_type=MESH,
        )

    def hand_on(buf, lane, blk):
        await_bytes(buf, hop_recv.at[lane])
        slab = pl.ds(pl.multiple_of(xor(blk // GROUP, route, groups.bit_length() - 1) * span, span), span)
        pltpu.make_async_remote_copy(
            src_ref=buf, dst_ref=pass_hbm.at[0, :, slab],
            send_sem=hop_send.at[lane], recv_sem=pass_recv.at[route],
            device_id={"section": goal, "blk": blk}, device_id_type=MESH,
        ).start()

    def hand_all_on():
        @pl.when(near)
        def _():
            hand_on(hop_near, 0, me)

        @pl.when(beside)
        def _():
            hand_on(hop_side, 1, me + 1)

    @pl.when((part == 1) & (route < half - 1))
    def _():
        hand_all_on()

    await_bytes(values, v_recv)
    await_bytes(keys, k_recv)

    def attend(g):
        here = pl.ds(pl.multiple_of(g * GROUP * rows, GROUP * rows), GROUP * rows)
        scores = lax.dot_general(
            queries[here], keys[...], (((1,), (1,)), ((), ())), preferred_element_type=jnp.float32
        )
        scores = scores * scale + bias
        weights = jnp.exp2(scores - jnp.max(scores, axis=-1, keepdims=True))
        total = jnp.sum(weights, axis=-1, keepdims=True)
        product = jnp.dot(weights.astype(jnp.bfloat16), values[...], preferred_element_type=jnp.float32)
        mixed[here] = (product / total).astype(jnp.bfloat16)

    def give_back(g):
        base = slab_base(g)
        place = attention.at[:, lanes(me)]
        for k in range(GROUP):
            out = mixed.at[token_rows(g * GROUP + k)]
            if k == 0:

                @pl.when(g > 0)
                def _(out=out):
                    send(out, place, o_send, o_recv.at[g], base)

                @pl.when(g == 0)
                def _(out=out):
                    own(out, place, o_recv.at[0])
            else:
                send(out, place, o_send, o_recv.at[g], partner_in(base, k))

    loads[3].wait()
    loads[4].wait()
    loads[8].wait()
    step = step_ref[0]

    def own_copy(slab, g):
        return pltpu.make_async_copy(layer_out.at[:, slab], out_hbm.at[0, :, slab], out_sem.at[g])

    def finish(g):
        await_bytes(mixed.at[pl.ds(0, GROUP * rows)], o_recv.at[g])
        slab = slab_of(g)
        gate = table[pl.ds(step, 1), slab]
        mix = attention[:, slab].astype(jnp.float32)
        layer_out[:, slab] = (acts[:, slab].astype(jnp.float32) + gate * mix).astype(jnp.bfloat16)
        direct = (route < half - 1) | (g == half - 1)

        @pl.when(direct)
        def _():
            pass_copy(slab, g, after).start()

        indirect = jnp.logical_not(direct)
        aside = turned(spot, part)

        @pl.when(indirect & jnp.logical_not(aside))
        def _():
            hop_copy(slab, g, hop_near, 0, me).start()

        @pl.when(indirect & aside)
        def _():
            hop_copy(slab, g, hop_side, 1, me - 1).start()

        own_copy(slab, g).start()

    def next_group(g):
        await_bytes(queries.at[pl.ds(0, GROUP * rows)], q_recv.at[g])
        attend(g)
        give_back(g)

    lag = jnp.where(far, min(LAG, groups), min(WAIT, groups))

    def early(p, c):
        next_group(p)
        return c

    def hand_on_after(g):
        @pl.when((part == 0) & (route < half - 1) & (g == jnp.minimum(route + DEFER, groups - 1)))
        def _():
            hand_all_on()

    def both(p, c):
        next_group(p)
        finish(p - lag)
        hand_on_after(p - lag)
        return c

    def late(p, c):
        finish(p)
        hand_on_after(p)
        return c

    lax.fori_loop(0, lag, early, 0)

    calls = jnp.where(far, 1, served)

    @pl.when((part == 0) & (calls > 0))
    def _():
        pl.semaphore_wait(go, calls)

    lax.fori_loop(lag, groups, both, 0)
    lax.fori_loop(groups - lag, groups, late, 0)

    @pl.when(sec < sections - 1)
    def _():
        if QWAIT < 1:
            await_bytes(values.at[others], v_send)
        if QWAIT < 2:
            await_bytes(values.at[others], k_send)
        await_bytes(values.at[others], q_send)

    await_bytes(values.at[others], o_send)

    @pl.when(helper & near)
    def _():
        await_bytes(hop_near, hop_send.at[0])

    @pl.when(helper & beside)
    def _():
        await_bytes(hop_side, hop_send.at[1])

    def settle(g, c):
        slab = slab_of(g)
        own_copy(slab, g).wait()
        pass_copy(slab, g, after).wait()
        return c

    lax.fori_loop(0, groups, settle, 0)


def body(acts, q_in, k_in, v_in, modulation, q_gain, k_gain, patch_len, timestep):
    n = lax.axis_size("blk")
    sections = lax.axis_size("section")
    _, rows, channels = acts.shape
    groups = n // GROUP
    whole = pltpu.VMEM((rows, channels), jnp.bfloat16)
    owned = pltpu.VMEM((n * rows, HEAD), jnp.bfloat16)
    out = jax.ShapeDtypeStruct(acts.shape, jnp.bfloat16)
    dma = pltpu.SemaphoreType.DMA
    return pl.pallas_call(
        functools.partial(kernel, n, sections),
        out_shape=(out, out),
        in_specs=[pl.BlockSpec(memory_space=pltpu.MemorySpace.HBM)] * 9,
        out_specs=[pl.BlockSpec(memory_space=pl.ANY)] * 2,
        scratch_shapes=[
            whole, whole, whole, whole,
            pltpu.VMEM(modulation.shape[1:], jnp.float32),
            pltpu.VMEM((1, channels), jnp.float32),
            pltpu.VMEM((1, channels), jnp.float32),
            pltpu.SMEM((1,), jnp.int32),
            pltpu.SMEM((1,), jnp.int32),
            whole, whole, owned, owned, owned, owned, whole, whole,
            dma((9,)), dma, dma, dma, dma, dma, dma,
            dma((groups,)), dma((groups,)), dma((groups,)), dma((groups,)), dma((groups,)),
            pltpu.VMEM((rows, GROUP * HEAD), jnp.bfloat16),
            pltpu.VMEM((rows, GROUP * HEAD), jnp.bfloat16),
            dma((2,)), dma((2,)),
            pltpu.SemaphoreType.REGULAR, pltpu.SemaphoreType.REGULAR,
        ],
        compiler_params=pltpu.CompilerParams(
            collective_id=0, has_side_effects=True, vmem_limit_bytes=60 << 20
        ),
        name="relay_attention",
    )(acts, q_in, k_in, v_in, modulation, q_gain, k_gain, patch_len, timestep)


def solution(mesh):
    return jax.shard_map(
        body,
        mesh=mesh,
        in_specs=(
            P("section", "blk", None),
            P("section", "blk", None),
            P("section", "blk", None),
            P("section", "blk", None),
            P("section", None, None),
            P("section", None),
            P("section", None),
            P("section"),
            P(),
        ),
        out_specs=(P("section", "blk", None), P("section", "blk", None)),
        check_vma=False,
    )
```

```python
import functools
import math

import jax
import jax.numpy as jnp
from jax import lax
from jax.experimental import pallas as pl
from jax.experimental.pallas import tpu as pltpu
from jax.sharding import PartitionSpec as P

HEAD = 128
GROUP = 4
RUN = 8
LAG = 8
WAIT = 8
DEFER = 2
QWAIT = 0
INNER = 8
MESH = pl.DeviceIdType.MESH


def xor(a, b, bits):
    return sum((((a // 2**i) + (b // 2**i)) % 2) * 2**i for i in range(bits))


def kernel(
    n, sections,
    acts_hbm, q_hbm, k_hbm, v_hbm, mod_hbm, q_gain_hbm, k_gain_hbm, length_hbm, step_hbm,
    out_hbm, pass_hbm,
    acts, q_raw, k_raw, v_raw, table, q_gain, k_gain, length_ref, step_ref, q_unit, k_unit, keys, values, queries, mixed, attention, layer_out,
    load_sem, v_send, k_send, q_send, o_send, v_recv, k_recv, q_recv, o_recv, pass_send, pass_recv, out_sem, hop_near, hop_side, hop_send, hop_recv, go, turn,
):
    bits = n.bit_length() - 1
    groups = n // GROUP
    rows = acts.shape[0]
    span = GROUP * HEAD
    me = lax.axis_index("blk")
    sec = lax.axis_index("section")
    after = (sec + 1) % sections
    before = (sec + sections - 1) % sections

    barrier = pltpu.get_barrier_semaphore()

    flip = [(1 - 2 * ((me // 2**i) % 2)) * 2**i for i in range(bits)]
    inner = min(INNER, n)
    low = inner.bit_length() - 1
    low_group = GROUP.bit_length() - 1

    def flipped(base, first, count, which):
        for i in range(count):
            base = base + flip[first + i] * ((which // 2**i) % 2)
        return base

    def partner_in(base, j):
        return sum((flip[i] for i in range(low) if j >> i & 1), base)

    def each_partner(deliver):
        def block(hi, c):
            base = flipped(me, low, bits - low, hi)
            for j in sorted(range(inner), key=lambda j: (j % (inner // 2), -j)):
                if j == 0:

                    @pl.when(hi > 0)
                    def _():
                        deliver(hi * inner, base)
                else:
                    deliver(hi * inner + j, partner_in(base, j))
            return c

        lax.fori_loop(0, n // inner, block, 0)

    def greet(t, partner):
        pl.semaphore_signal(barrier, inc=1, device_id={"section": sec, "blk": partner}, device_id_type=MESH)

    def signal(sem, section, blk):
        pl.semaphore_signal(sem, inc=1, device_id={"section": section, "blk": blk}, device_id_type=MESH)

    half = sections // 2
    part = sec // half
    route = sec % half
    far = route == half - 1
    helper = route < half - 1
    goal = (part + 1) % 2 * half
    source = part * half + half - 1
    odd = sec % 2
    run = min(RUN, n)
    spot = me % run

    def turned(place, side):
        late = (place >= run // 2) & (place < run)
        return late & ((side == 0) | (place % 4 >= 2))

    def relay_blk(side):
        return me - jnp.where(turned(spot, side), 1, 0)

    near = jnp.logical_not(turned(spot, part))
    beside = turned(spot + 1, part)
    served = jnp.where(near, 1, 0) + jnp.where(beside, 1, 0)

    loads = [
        pltpu.make_async_copy(src.at[0], dst, load_sem.at[i])
        for i, (src, dst) in enumerate(
            ((v_hbm, v_raw), (k_hbm, k_raw), (q_hbm, q_raw), (acts_hbm, acts), (mod_hbm, table))
        )
    ]
    loads += [
        pltpu.make_async_copy(src, dst, load_sem.at[5 + i])
        for i, (src, dst) in enumerate(
            ((k_gain_hbm, k_gain), (q_gain_hbm, q_gain), (length_hbm, length_ref), (step_hbm, step_ref))
        )
    ]
    loads[0].start()
    each_partner(greet)
    for load in loads[1:]:
        load.start()

    @pl.when(odd == 0)
    def _():
        signal(barrier, after, me)

    @pl.when(route > 0)
    def _():
        signal(barrier, before, me)

    @pl.when(helper & near)
    def _():
        signal(barrier, source, me)

    @pl.when(helper & beside)
    def _():
        signal(barrier, source, me + 1)

    @pl.when((part == 0) & (near | far))
    def _():
        signal(barrier, goal, me)

    @pl.when((part == 0) & helper & beside)
    def _():
        signal(barrier, goal, me + 1)

    @pl.when(sec == 0)
    def _():
        def call(r, c):
            signal(barrier, half + r, relay_blk(1))
            return c

        lax.fori_loop(0, half - 1, call, 0)
        signal(barrier, sections - 1, me)

    expected = n - 1 + odd
    expected += jnp.where(far, half - 1, 1)
    expected += jnp.where(part == 1, jnp.where(far, 1, served), 0)
    expected += jnp.where(sec == half, half, 0)

    def unit(raw, gain, out):
        block = raw[...].astype(jnp.float32)
        scaled = block * lax.rsqrt(jnp.mean(block * block, axis=-1, keepdims=True) + 1e-06)
        out[...] = (scaled * gain[...]).astype(jnp.bfloat16)

    def lanes(head):
        return pl.ds(pl.multiple_of(head * HEAD, HEAD), HEAD)

    def token_rows(block):
        return pl.ds(pl.multiple_of(block * rows, rows), rows)

    mine = token_rows(me)

    def send(src, dst, send_sem, recv_sem, partner):
        pltpu.make_async_remote_copy(
            src_ref=src, dst_ref=dst, send_sem=send_sem, recv_sem=recv_sem,
            device_id={"section": sec, "blk": partner}, device_id_type=MESH,
        ).start()

    def await_bytes(ref, sem):
        pltpu.make_async_copy(ref, ref, sem).wait()

    loads[0].wait()
    pl.semaphore_wait(barrier, expected)

    @pl.when(sec == half)
    def _():
        def call(r, c):
            signal(go, r, relay_blk(0))
            return c

        lax.fori_loop(0, half - 1, call, 0)
        signal(go, half - 1, me)

    @pl.when(sec == sections - 2)
    def _():
        pl.semaphore_wait(turn, 1)

    def send_v(t, partner):
        send(v_raw.at[:, lanes(partner)], values.at[mine], v_send, v_recv, partner)

    def send_k(t, partner):
        send(k_unit.at[:, lanes(partner)], keys.at[mine], k_send, k_recv, partner)

    def send_q(t, partner):
        send(q_unit.at[:, lanes(partner)], queries.at[token_rows(t)], q_send, q_recv.at[t // GROUP], partner)

    def own(src, dst, sem):
        pltpu.make_async_copy(src, dst, sem).start()

    each_partner(send_v)
    loads[1].wait()
    loads[5].wait()
    unit(k_raw, k_gain, k_unit)
    each_partner(send_k)
    loads[2].wait()
    loads[6].wait()
    unit(q_raw, q_gain, q_unit)
    others = pl.ds(0, (n - 1) * rows)
    if QWAIT > 0:
        await_bytes(values.at[others], v_send)
    if QWAIT > 1:
        await_bytes(values.at[others], k_send)
    each_partner(send_q)
    own(v_raw.at[:, lanes(me)], values.at[mine], v_recv)
    own(k_unit.at[:, lanes(me)], keys.at[mine], k_recv)
    own(q_unit.at[:, lanes(me)], queries.at[pl.ds(0, rows)], q_recv.at[0])

    place = lax.broadcasted_iota(jnp.int32, (1, n * rows), 1)
    loads[7].wait()
    bias = jnp.where(place < length_ref[0], 0.0, -1e30)
    scale = math.log2(math.e) / math.sqrt(HEAD)
    @pl.when(sec == sections - 1)
    def _():
        if QWAIT < 1:
            await_bytes(values.at[others], v_send)
        if QWAIT < 2:
            await_bytes(values.at[others], k_send)
        await_bytes(values.at[others], q_send)
        signal(turn, before, me)

    def slab_base(g):
        return flipped(me, low_group, bits - low_group, g)

    def slab_of(g):
        return pl.ds(pl.multiple_of(slab_base(g) // GROUP * span, span), span)

    def pass_copy(slab, g, section):
        return pltpu.make_async_remote_copy(
            src_ref=layer_out.at[:, slab], dst_ref=pass_hbm.at[0, :, slab],
            send_sem=pass_send.at[g], recv_sem=pass_recv.at[g],
            device_id={"section": section, "blk": me}, device_id_type=MESH,
        )

    def hop_copy(slab, g, buf, lane, blk):
        return pltpu.make_async_remote_copy(
            src_ref=layer_out.at[:, slab], dst_ref=buf,
            send_sem=pass_send.at[g], recv_sem=hop_recv.at[lane],
            device_id={"section": part * half + g, "blk": blk}, device_id_type=MESH,
        )

    def hand_on(buf, lane, blk):
        await_bytes(buf, hop_recv.at[lane])
        slab = pl.ds(pl.multiple_of(xor(blk // GROUP, route, groups.bit_length() - 1) * span, span), span)
        pltpu.make_async_remote_copy(
            src_ref=buf, dst_ref=pass_hbm.at[0, :, slab],
            send_sem=hop_send.at[lane], recv_sem=pass_recv.at[route],
            device_id={"section": goal, "blk": blk}, device_id_type=MESH,
        ).start()

    def hand_all_on():
        @pl.when(near)
        def _():
            hand_on(hop_near, 0, me)

        @pl.when(beside)
        def _():
            hand_on(hop_side, 1, me + 1)

    @pl.when((part == 1) & (route < half - 1))
    def _():
        hand_all_on()

    await_bytes(values, v_recv)
    await_bytes(keys, k_recv)

    def attend(g):
        here = pl.ds(pl.multiple_of(g * GROUP * rows, GROUP * rows), GROUP * rows)
        scores = lax.dot_general(
            queries[here], keys[...], (((1,), (1,)), ((), ())), preferred_element_type=jnp.float32
        )
        scores = scores * scale + bias
        weights = jnp.exp2(scores - jnp.max(scores, axis=-1, keepdims=True))
        total = jnp.sum(weights, axis=-1, keepdims=True)
        product = jnp.dot(weights.astype(jnp.bfloat16), values[...], preferred_element_type=jnp.float32)
        mixed[here] = (product / total).astype(jnp.bfloat16)

    def give_back(g):
        base = slab_base(g)
        place = attention.at[:, lanes(me)]
        for k in range(GROUP):
            out = mixed.at[token_rows(g * GROUP + k)]
            if k == 0:

                @pl.when(g > 0)
                def _(out=out):
                    send(out, place, o_send, o_recv.at[g], base)

                @pl.when(g == 0)
                def _(out=out):
                    own(out, place, o_recv.at[0])
            else:
                send(out, place, o_send, o_recv.at[g], partner_in(base, k))

    loads[3].wait()
    loads[4].wait()
    loads[8].wait()
    step = step_ref[0]

    def own_copy(slab, g):
        return pltpu.make_async_copy(layer_out.at[:, slab], out_hbm.at[0, :, slab], out_sem.at[g])

    def finish(g):
        await_bytes(mixed.at[pl.ds(0, GROUP * rows)], o_recv.at[g])
        slab = slab_of(g)
        gate = table[pl.ds(step, 1), slab]
        mix = attention[:, slab].astype(jnp.float32)
        layer_out[:, slab] = (acts[:, slab].astype(jnp.float32) + gate * mix).astype(jnp.bfloat16)
        direct = (route < half - 1) | (g == half - 1)

        @pl.when(direct)
        def _():
            pass_copy(slab, g, after).start()

        indirect = jnp.logical_not(direct)
        aside = turned(spot, part)

        @pl.when(indirect & jnp.logical_not(aside))
        def _():
            hop_copy(slab, g, hop_near, 0, me).start()

        @pl.when(indirect & aside)
        def _():
            hop_copy(slab, g, hop_side, 1, me - 1).start()

        own_copy(slab, g).start()

    def next_group(g):
        await_bytes(queries.at[pl.ds(0, GROUP * rows)], q_recv.at[g])
        attend(g)
        give_back(g)

    lag = jnp.where(far, min(LAG, groups), min(WAIT, groups))

    def early(p, c):
        next_group(p)
        return c

    def hand_on_after(g):
        @pl.when((part == 0) & (route < half - 1) & (g == jnp.minimum(route + DEFER, groups - 1)))
        def _():
            hand_all_on()

    def both(p, c):
        next_group(p)
        finish(p - lag)
        hand_on_after(p - lag)
        return c

    def late(p, c):
        finish(p)
        hand_on_after(p)
        return c

    lax.fori_loop(0, lag, early, 0)

    calls = jnp.where(far, 1, served)

    @pl.when((part == 0) & (calls > 0))
    def _():
        pl.semaphore_wait(go, calls)

    lax.fori_loop(lag, groups, both, 0)
    lax.fori_loop(groups - lag, groups, late, 0)

    @pl.when(sec < sections - 1)
    def _():
        if QWAIT < 1:
            await_bytes(values.at[others], v_send)
        if QWAIT < 2:
            await_bytes(values.at[others], k_send)
        await_bytes(values.at[others], q_send)

    await_bytes(values.at[others], o_send)

    @pl.when(helper & near)
    def _():
        await_bytes(hop_near, hop_send.at[0])

    @pl.when(helper & beside)
    def _():
        await_bytes(hop_side, hop_send.at[1])

    def settle(g, c):
        slab = slab_of(g)
        own_copy(slab, g).wait()
        pass_copy(slab, g, after).wait()
        return c

    lax.fori_loop(0, groups, settle, 0)


def body(acts, q_in, k_in, v_in, modulation, q_gain, k_gain, patch_len, timestep):
    n = lax.axis_size("blk")
    sections = lax.axis_size("section")
    _, rows, channels = acts.shape
    groups = n // GROUP
    whole = pltpu.VMEM((rows, channels), jnp.bfloat16)
    owned = pltpu.VMEM((n * rows, HEAD), jnp.bfloat16)
    out = jax.ShapeDtypeStruct(acts.shape, jnp.bfloat16)
    dma = pltpu.SemaphoreType.DMA
    kept, sent = pl.pallas_call(
        functools.partial(kernel, n, sections),
        out_shape=(out, out),
        in_specs=[pl.BlockSpec(memory_space=pltpu.MemorySpace.HBM)] * 9,
        out_specs=[pl.BlockSpec(memory_space=pl.ANY)] * 2,
        scratch_shapes=[
            whole, whole, whole, whole,
            pltpu.VMEM(modulation.shape[1:], jnp.float32),
            pltpu.VMEM((1, channels), jnp.float32),
            pltpu.VMEM((1, channels), jnp.float32),
            pltpu.SMEM((1,), jnp.int32),
            pltpu.SMEM((1,), jnp.int32),
            whole, whole, owned, owned, owned, owned, whole, whole,
            dma((9,)), dma, dma, dma, dma, dma, dma,
            dma((groups,)), dma((groups,)), dma((groups,)), dma((groups,)), dma((groups,)),
            pltpu.VMEM((rows, GROUP * HEAD), jnp.bfloat16),
            pltpu.VMEM((rows, GROUP * HEAD), jnp.bfloat16),
            dma((2,)), dma((2,)),
            pltpu.SemaphoreType.REGULAR, pltpu.SemaphoreType.REGULAR,
        ],
        compiler_params=pltpu.CompilerParams(
            collective_id=0, has_side_effects=True, vmem_limit_bytes=60 << 20
        ),
        name="relay_attention",
    )(acts, q_in, k_in, v_in, modulation, q_gain, k_gain, patch_len, timestep)

    def place(kept_in, sent_in, kept_out, sent_out, kept_buf, sent_buf, sems):
        reads = [
            pltpu.make_async_copy(kept_in, kept_buf, sems.at[0]),
            pltpu.make_async_copy(sent_in, sent_buf, sems.at[1]),
        ]
        writes = [
            pltpu.make_async_copy(kept_buf, kept_out, sems.at[2]),
            pltpu.make_async_copy(sent_buf, sent_out, sems.at[3]),
        ]
        for copy in reads:
            copy.start()
        for read, write in zip(reads, writes):
            read.wait()
            write.start()
        for copy in writes:
            copy.wait()

    return pl.pallas_call(
        place,
        out_shape=(out, out),
        in_specs=[pl.BlockSpec(memory_space=pl.ANY)] * 2,
        out_specs=[pl.BlockSpec(memory_space=pl.ANY)] * 2,
        scratch_shapes=[pltpu.VMEM(acts.shape, jnp.bfloat16)] * 2 + [dma((4,))],
        compiler_params=pltpu.CompilerParams(vmem_limit_bytes=60 << 20),
        name="place",
    )(kept, sent)


def solution(mesh):
    return jax.shard_map(
        body,
        mesh=mesh,
        in_specs=(
            P("section", "blk", None),
            P("section", "blk", None),
            P("section", "blk", None),
            P("section", "blk", None),
            P("section", None, None),
            P("section", None),
            P("section", None),
            P("section"),
            P(),
        ),
        out_specs=(P("section", "blk", None), P("section", "blk", None)),
        check_vma=False,
    )
```

```python
import functools
import math

import jax
import jax.numpy as jnp
from jax import lax
from jax.experimental import pallas as pl
from jax.experimental.pallas import tpu as pltpu
from jax.sharding import PartitionSpec as P

HEAD = 128
GROUP = 4
RUN = 8
LAG = 8
WAIT = 8
DEFER = 2
QWAIT = 0
INNER = 8
MESH = pl.DeviceIdType.MESH


def xor(a, b, bits):
    return sum((((a // 2**i) + (b // 2**i)) % 2) * 2**i for i in range(bits))


def kernel(
    n, sections,
    acts_hbm, q_hbm, k_hbm, v_hbm, mod_hbm, q_gain_hbm, k_gain_hbm, length_hbm, step_hbm,
    out_hbm, pass_hbm,
    acts, q_raw, k_raw, v_raw, table, q_gain, k_gain, length_ref, step_ref, q_unit, k_unit, keys, values, queries, mixed, attention, layer_out,
    load_sem, v_send, k_send, q_send, o_send, v_recv, k_recv, q_recv, o_recv, pass_send, pass_recv, out_sem, hop_near, hop_side, hop_send, hop_recv, go, turn,
):
    bits = n.bit_length() - 1
    groups = n // GROUP
    rows = acts.shape[0]
    span = GROUP * HEAD
    me = lax.axis_index("blk")
    sec = lax.axis_index("section")
    after = (sec + 1) % sections
    before = (sec + sections - 1) % sections

    barrier = pltpu.get_barrier_semaphore()

    flip = [(1 - 2 * ((me // 2**i) % 2)) * 2**i for i in range(bits)]
    inner = min(INNER, n)
    low = inner.bit_length() - 1
    low_group = GROUP.bit_length() - 1

    def flipped(base, first, count, which):
        for i in range(count):
            base = base + flip[first + i] * ((which // 2**i) % 2)
        return base

    def partner_in(base, j):
        return sum((flip[i] for i in range(low) if j >> i & 1), base)

    def each_partner(deliver, shift=0):
        def block(i, c):
            hi = (i + shift) % (n // inner)
            base = flipped(me, low, bits - low, hi)
            for j in sorted(range(inner), key=lambda j: (j % (inner // 2), -j)):
                if j == 0:

                    @pl.when(hi > 0)
                    def _():
                        deliver(hi * inner, base)
                else:
                    deliver(hi * inner + j, partner_in(base, j))
            return c

        lax.fori_loop(0, n // inner, block, 0)

    def greet(t, partner):
        pl.semaphore_signal(barrier, inc=1, device_id={"section": sec, "blk": partner}, device_id_type=MESH)

    def signal(sem, section, blk):
        pl.semaphore_signal(sem, inc=1, device_id={"section": section, "blk": blk}, device_id_type=MESH)

    half = sections // 2
    part = sec // half
    route = sec % half
    far = route == half - 1
    helper = route < half - 1
    goal = (part + 1) % 2 * half
    source = part * half + half - 1
    odd = sec % 2
    run = min(RUN, n)
    spot = me % run

    def turned(place, side):
        late = (place >= run // 2) & (place < run)
        return late & ((side == 0) | (place % 4 >= 2))

    def relay_blk(side):
        return me - jnp.where(turned(spot, side), 1, 0)

    near = jnp.logical_not(turned(spot, part))
    beside = turned(spot + 1, part)
    served = jnp.where(near, 1, 0) + jnp.where(beside, 1, 0)

    loads = [
        pltpu.make_async_copy(src.at[0], dst, load_sem.at[i])
        for i, (src, dst) in enumerate(
            ((v_hbm, v_raw), (k_hbm, k_raw), (q_hbm, q_raw), (acts_hbm, acts), (mod_hbm, table))
        )
    ]
    loads += [
        pltpu.make_async_copy(src, dst, load_sem.at[5 + i])
        for i, (src, dst) in enumerate(
            ((k_gain_hbm, k_gain), (q_gain_hbm, q_gain), (length_hbm, length_ref), (step_hbm, step_ref))
        )
    ]
    loads[0].start()
    each_partner(greet)
    for load in loads[1:]:
        load.start()

    @pl.when(odd == 0)
    def _():
        signal(barrier, after, me)

    @pl.when(route > 0)
    def _():
        signal(barrier, before, me)

    @pl.when(helper & near)
    def _():
        signal(barrier, source, me)

    @pl.when(helper & beside)
    def _():
        signal(barrier, source, me + 1)

    @pl.when((part == 0) & (near | far))
    def _():
        signal(barrier, goal, me)

    @pl.when((part == 0) & helper & beside)
    def _():
        signal(barrier, goal, me + 1)

    @pl.when(sec == 0)
    def _():
        def call(r, c):
            signal(barrier, half + r, relay_blk(1))
            return c

        lax.fori_loop(0, half - 1, call, 0)
        signal(barrier, sections - 1, me)

    expected = n - 1 + odd
    expected += jnp.where(far, half - 1, 1)
    expected += jnp.where(part == 1, jnp.where(far, 1, served), 0)
    expected += jnp.where(sec == half, half, 0)

    def unit(raw, gain, out):
        block = raw[...].astype(jnp.float32)
        scaled = block * lax.rsqrt(jnp.mean(block * block, axis=-1, keepdims=True) + 1e-06)
        out[...] = (scaled * gain[...]).astype(jnp.bfloat16)

    def lanes(head):
        return pl.ds(pl.multiple_of(head * HEAD, HEAD), HEAD)

    def token_rows(block):
        return pl.ds(pl.multiple_of(block * rows, rows), rows)

    mine = token_rows(me)

    def send(src, dst, send_sem, recv_sem, partner):
        pltpu.make_async_remote_copy(
            src_ref=src, dst_ref=dst, send_sem=send_sem, recv_sem=recv_sem,
            device_id={"section": sec, "blk": partner}, device_id_type=MESH,
        ).start()

    def await_bytes(ref, sem):
        pltpu.make_async_copy(ref, ref, sem).wait()

    loads[0].wait()
    pl.semaphore_wait(barrier, expected)

    @pl.when(sec == half)
    def _():
        def call(r, c):
            signal(go, r, relay_blk(0))
            return c

        lax.fori_loop(0, half - 1, call, 0)
        signal(go, half - 1, me)

    @pl.when(sec == sections - 2)
    def _():
        pl.semaphore_wait(turn, 1)

    def send_v(t, partner):
        send(v_raw.at[:, lanes(partner)], values.at[mine], v_send, v_recv, partner)

    def send_k(t, partner):
        send(k_unit.at[:, lanes(partner)], keys.at[mine], k_send, k_recv, partner)

    def send_q(t, partner):
        send(q_unit.at[:, lanes(partner)], queries.at[token_rows(t)], q_send, q_recv.at[t // GROUP], partner)

    def own(src, dst, sem):
        pltpu.make_async_copy(src, dst, sem).start()

    each_partner(send_v, odd * (n // inner // 2))
    loads[1].wait()
    loads[5].wait()
    unit(k_raw, k_gain, k_unit)
    each_partner(send_k, odd * (n // inner // 2))
    loads[2].wait()
    loads[6].wait()
    unit(q_raw, q_gain, q_unit)
    others = pl.ds(0, (n - 1) * rows)
    if QWAIT > 0:
        await_bytes(values.at[others], v_send)
    if QWAIT > 1:
        await_bytes(values.at[others], k_send)
    each_partner(send_q)
    own(v_raw.at[:, lanes(me)], values.at[mine], v_recv)
    own(k_unit.at[:, lanes(me)], keys.at[mine], k_recv)
    own(q_unit.at[:, lanes(me)], queries.at[pl.ds(0, rows)], q_recv.at[0])

    place = lax.broadcasted_iota(jnp.int32, (1, n * rows), 1)
    loads[7].wait()
    bias = jnp.where(place < length_ref[0], 0.0, -1e30)
    scale = math.log2(math.e) / math.sqrt(HEAD)
    @pl.when(sec == sections - 1)
    def _():
        if QWAIT < 1:
            await_bytes(values.at[others], v_send)
        if QWAIT < 2:
            await_bytes(values.at[others], k_send)
        await_bytes(values.at[others], q_send)
        signal(turn, before, me)

    def slab_base(g):
        return flipped(me, low_group, bits - low_group, g)

    def slab_of(g):
        return pl.ds(pl.multiple_of(slab_base(g) // GROUP * span, span), span)

    def pass_copy(slab, g, section):
        return pltpu.make_async_remote_copy(
            src_ref=layer_out.at[:, slab], dst_ref=pass_hbm.at[0, :, slab],
            send_sem=pass_send.at[g], recv_sem=pass_recv.at[g],
            device_id={"section": section, "blk": me}, device_id_type=MESH,
        )

    def hop_copy(slab, g, buf, lane, blk):
        return pltpu.make_async_remote_copy(
            src_ref=layer_out.at[:, slab], dst_ref=buf,
            send_sem=pass_send.at[g], recv_sem=hop_recv.at[lane],
            device_id={"section": part * half + g, "blk": blk}, device_id_type=MESH,
        )

    def hand_on(buf, lane, blk):
        await_bytes(buf, hop_recv.at[lane])
        slab = pl.ds(pl.multiple_of(xor(blk // GROUP, route, groups.bit_length() - 1) * span, span), span)
        pltpu.make_async_remote_copy(
            src_ref=buf, dst_ref=pass_hbm.at[0, :, slab],
            send_sem=hop_send.at[lane], recv_sem=pass_recv.at[route],
            device_id={"section": goal, "blk": blk}, device_id_type=MESH,
        ).start()

    def hand_all_on():
        @pl.when(near)
        def _():
            hand_on(hop_near, 0, me)

        @pl.when(beside)
        def _():
            hand_on(hop_side, 1, me + 1)

    @pl.when((part == 1) & (route < half - 1))
    def _():
        hand_all_on()

    await_bytes(values, v_recv)
    await_bytes(keys, k_recv)

    def attend(g):
        here = pl.ds(pl.multiple_of(g * GROUP * rows, GROUP * rows), GROUP * rows)
        scores = lax.dot_general(
            queries[here], keys[...], (((1,), (1,)), ((), ())), preferred_element_type=jnp.float32
        )
        scores = scores * scale + bias
        weights = jnp.exp2(scores - jnp.max(scores, axis=-1, keepdims=True))
        total = jnp.sum(weights, axis=-1, keepdims=True)
        product = jnp.dot(weights.astype(jnp.bfloat16), values[...], preferred_element_type=jnp.float32)
        mixed[here] = (product / total).astype(jnp.bfloat16)

    def give_back(g):
        base = slab_base(g)
        place = attention.at[:, lanes(me)]
        for k in range(GROUP):
            out = mixed.at[token_rows(g * GROUP + k)]
            if k == 0:

                @pl.when(g > 0)
                def _(out=out):
                    send(out, place, o_send, o_recv.at[g], base)

                @pl.when(g == 0)
                def _(out=out):
                    own(out, place, o_recv.at[0])
            else:
                send(out, place, o_send, o_recv.at[g], partner_in(base, k))

    loads[3].wait()
    loads[4].wait()
    loads[8].wait()
    step = step_ref[0]

    def own_copy(slab, g):
        return pltpu.make_async_copy(layer_out.at[:, slab], out_hbm.at[0, :, slab], out_sem.at[g])

    def finish(g):
        await_bytes(mixed.at[pl.ds(0, GROUP * rows)], o_recv.at[g])
        slab = slab_of(g)
        gate = table[pl.ds(step, 1), slab]
        mix = attention[:, slab].astype(jnp.float32)
        layer_out[:, slab] = (acts[:, slab].astype(jnp.float32) + gate * mix).astype(jnp.bfloat16)
        direct = (route < half - 1) | (g == half - 1)

        @pl.when(direct)
        def _():
            pass_copy(slab, g, after).start()

        indirect = jnp.logical_not(direct)
        aside = turned(spot, part)

        @pl.when(indirect & jnp.logical_not(aside))
        def _():
            hop_copy(slab, g, hop_near, 0, me).start()

        @pl.when(indirect & aside)
        def _():
            hop_copy(slab, g, hop_side, 1, me - 1).start()

        own_copy(slab, g).start()

    def next_group(g):
        await_bytes(queries.at[pl.ds(0, GROUP * rows)], q_recv.at[g])
        attend(g)
        give_back(g)

    lag = jnp.where(far, min(LAG, groups), min(WAIT, groups))

    def early(p, c):
        next_group(p)
        return c

    def hand_on_after(g):
        @pl.when((part == 0) & (route < half - 1) & (g == jnp.minimum(route + DEFER, groups - 1)))
        def _():
            hand_all_on()

    def both(p, c):
        next_group(p)
        finish(p - lag)
        hand_on_after(p - lag)
        return c

    def late(p, c):
        finish(p)
        hand_on_after(p)
        return c

    lax.fori_loop(0, lag, early, 0)

    calls = jnp.where(far, 1, served)

    @pl.when((part == 0) & (calls > 0))
    def _():
        pl.semaphore_wait(go, calls)

    lax.fori_loop(lag, groups, both, 0)
    lax.fori_loop(groups - lag, groups, late, 0)

    @pl.when(sec < sections - 1)
    def _():
        if QWAIT < 1:
            await_bytes(values.at[others], v_send)
        if QWAIT < 2:
            await_bytes(values.at[others], k_send)
        await_bytes(values.at[others], q_send)

    await_bytes(values.at[others], o_send)

    @pl.when(helper & near)
    def _():
        await_bytes(hop_near, hop_send.at[0])

    @pl.when(helper & beside)
    def _():
        await_bytes(hop_side, hop_send.at[1])

    def settle(g, c):
        slab = slab_of(g)
        own_copy(slab, g).wait()
        pass_copy(slab, g, after).wait()
        return c

    lax.fori_loop(0, groups, settle, 0)


def body(acts, q_in, k_in, v_in, modulation, q_gain, k_gain, patch_len, timestep):
    n = lax.axis_size("blk")
    sections = lax.axis_size("section")
    _, rows, channels = acts.shape
    groups = n // GROUP
    whole = pltpu.VMEM((rows, channels), jnp.bfloat16)
    owned = pltpu.VMEM((n * rows, HEAD), jnp.bfloat16)
    out = jax.ShapeDtypeStruct(acts.shape, jnp.bfloat16)
    dma = pltpu.SemaphoreType.DMA
    kept, sent = pl.pallas_call(
        functools.partial(kernel, n, sections),
        out_shape=(out, out),
        in_specs=[pl.BlockSpec(memory_space=pltpu.MemorySpace.HBM)] * 9,
        out_specs=[pl.BlockSpec(memory_space=pl.ANY)] * 2,
        scratch_shapes=[
            whole, whole, whole, whole,
            pltpu.VMEM(modulation.shape[1:], jnp.float32),
            pltpu.VMEM((1, channels), jnp.float32),
            pltpu.VMEM((1, channels), jnp.float32),
            pltpu.SMEM((1,), jnp.int32),
            pltpu.SMEM((1,), jnp.int32),
            whole, whole, owned, owned, owned, owned, whole, whole,
            dma((9,)), dma, dma, dma, dma, dma, dma,
            dma((groups,)), dma((groups,)), dma((groups,)), dma((groups,)), dma((groups,)),
            pltpu.VMEM((rows, GROUP * HEAD), jnp.bfloat16),
            pltpu.VMEM((rows, GROUP * HEAD), jnp.bfloat16),
            dma((2,)), dma((2,)),
            pltpu.SemaphoreType.REGULAR, pltpu.SemaphoreType.REGULAR,
        ],
        compiler_params=pltpu.CompilerParams(
            collective_id=0, has_side_effects=True, vmem_limit_bytes=60 << 20
        ),
        name="relay_attention",
    )(acts, q_in, k_in, v_in, modulation, q_gain, k_gain, patch_len, timestep)

    def place(kept_in, sent_in, kept_out, sent_out, kept_buf, sent_buf, sems):
        reads = [
            pltpu.make_async_copy(kept_in, kept_buf, sems.at[0]),
            pltpu.make_async_copy(sent_in, sent_buf, sems.at[1]),
        ]
        writes = [
            pltpu.make_async_copy(kept_buf, kept_out, sems.at[2]),
            pltpu.make_async_copy(sent_buf, sent_out, sems.at[3]),
        ]
        for copy in reads:
            copy.start()
        for read, write in zip(reads, writes):
            read.wait()
            write.start()
        for copy in writes:
            copy.wait()

    return pl.pallas_call(
        place,
        out_shape=(out, out),
        in_specs=[pl.BlockSpec(memory_space=pl.ANY)] * 2,
        out_specs=[pl.BlockSpec(memory_space=pl.ANY)] * 2,
        scratch_shapes=[pltpu.VMEM(acts.shape, jnp.bfloat16)] * 2 + [dma((4,))],
        compiler_params=pltpu.CompilerParams(vmem_limit_bytes=60 << 20),
        name="place",
    )(kept, sent)


def solution(mesh):
    return jax.shard_map(
        body,
        mesh=mesh,
        in_specs=(
            P("section", "blk", None),
            P("section", "blk", None),
            P("section", "blk", None),
            P("section", "blk", None),
            P("section", None, None),
            P("section", None),
            P("section", None),
            P("section"),
            P(),
        ),
        out_specs=(P("section", "blk", None), P("section", "blk", None)),
        check_vma=False,
    )
```

```python
import functools
import math

import jax
import jax.numpy as jnp
from jax import lax
from jax.experimental import pallas as pl
from jax.experimental.pallas import tpu as pltpu
from jax.sharding import PartitionSpec as P

HEAD = 128
GROUP = 4
RUN = 8
LAG = 8
WAIT = 8
DEFER = 1
QWAIT = 0
INNER = 8
MESH = pl.DeviceIdType.MESH


def xor(a, b, bits):
    return sum((((a // 2**i) + (b // 2**i)) % 2) * 2**i for i in range(bits))


def kernel(
    n, sections,
    acts_hbm, q_hbm, k_hbm, v_hbm, mod_hbm, q_gain_hbm, k_gain_hbm, length_hbm, step_hbm,
    out_hbm, pass_hbm,
    acts, q_raw, k_raw, v_raw, table, q_gain, k_gain, length_ref, step_ref, q_unit, k_unit, keys, values, queries, mixed, attention, layer_out,
    load_sem, v_send, k_send, q_send, o_send, v_recv, k_recv, q_recv, o_recv, pass_send, pass_recv, out_sem, hop_near, hop_side, hop_send, hop_recv, go, turn,
):
    bits = n.bit_length() - 1
    groups = n // GROUP
    rows = acts.shape[0]
    span = GROUP * HEAD
    me = lax.axis_index("blk")
    sec = lax.axis_index("section")
    after = (sec + 1) % sections
    before = (sec + sections - 1) % sections

    barrier = pltpu.get_barrier_semaphore()

    flip = [(1 - 2 * ((me // 2**i) % 2)) * 2**i for i in range(bits)]
    inner = min(INNER, n)
    low = inner.bit_length() - 1
    low_group = GROUP.bit_length() - 1

    def flipped(base, first, count, which):
        for i in range(count):
            base = base + flip[first + i] * ((which // 2**i) % 2)
        return base

    def partner_in(base, j):
        return sum((flip[i] for i in range(low) if j >> i & 1), base)

    def each_partner(deliver, shift=0):
        def block(i, c):
            hi = (i + shift) % (n // inner)
            base = flipped(me, low, bits - low, hi)
            for j in sorted(range(inner), key=lambda j: (j % (inner // 2), -j)):
                if j == 0:

                    @pl.when(hi > 0)
                    def _():
                        deliver(hi * inner, base)
                else:
                    deliver(hi * inner + j, partner_in(base, j))
            return c

        lax.fori_loop(0, n // inner, block, 0)

    def greet(t, partner):
        pl.semaphore_signal(barrier, inc=1, device_id={"section": sec, "blk": partner}, device_id_type=MESH)

    def signal(sem, section, blk):
        pl.semaphore_signal(sem, inc=1, device_id={"section": section, "blk": blk}, device_id_type=MESH)

    half = sections // 2
    part = sec // half
    route = sec % half
    far = route == half - 1
    helper = route < half - 1
    goal = (part + 1) % 2 * half
    source = part * half + half - 1
    odd = sec % 2
    run = min(RUN, n)
    spot = me % run

    def turned(place, side):
        late = (place >= run // 2) & (place < run)
        return late & ((side == 0) | ((place % 4 >= 2) | (place == 5)))

    def relay_blk(side):
        return me - jnp.where(turned(spot, side), 1, 0)

    near = jnp.logical_not(turned(spot, part))
    beside = turned(spot + 1, part)
    served = jnp.where(near, 1, 0) + jnp.where(beside, 1, 0)

    loads = [
        pltpu.make_async_copy(src.at[0], dst, load_sem.at[i])
        for i, (src, dst) in enumerate(
            ((v_hbm, v_raw), (k_hbm, k_raw), (q_hbm, q_raw), (acts_hbm, acts), (mod_hbm, table))
        )
    ]
    loads += [
        pltpu.make_async_copy(src, dst, load_sem.at[5 + i])
        for i, (src, dst) in enumerate(
            ((k_gain_hbm, k_gain), (q_gain_hbm, q_gain), (length_hbm, length_ref), (step_hbm, step_ref))
        )
    ]
    loads[0].start()
    each_partner(greet)
    for load in loads[1:]:
        load.start()

    @pl.when(odd == 0)
    def _():
        signal(barrier, after, me)

    @pl.when(route > 0)
    def _():
        signal(barrier, before, me)

    @pl.when(helper & near)
    def _():
        signal(barrier, source, me)

    @pl.when(helper & beside)
    def _():
        signal(barrier, source, me + 1)

    @pl.when((part == 0) & (near | far))
    def _():
        signal(barrier, goal, me)

    @pl.when((part == 0) & helper & beside)
    def _():
        signal(barrier, goal, me + 1)

    @pl.when(sec == 0)
    def _():
        def call(r, c):
            signal(barrier, half + r, relay_blk(1))
            return c

        lax.fori_loop(0, half - 1, call, 0)
        signal(barrier, sections - 1, me)

    expected = n - 1 + odd
    expected += jnp.where(far, half - 1, 1)
    expected += jnp.where(part == 1, jnp.where(far, 1, served), 0)
    expected += jnp.where(sec == half, half, 0)

    def unit(raw, gain, out):
        block = raw[...].astype(jnp.float32)
        scaled = block * lax.rsqrt(jnp.mean(block * block, axis=-1, keepdims=True) + 1e-06)
        out[...] = (scaled * gain[...]).astype(jnp.bfloat16)

    def lanes(head):
        return pl.ds(pl.multiple_of(head * HEAD, HEAD), HEAD)

    def token_rows(block):
        return pl.ds(pl.multiple_of(block * rows, rows), rows)

    mine = token_rows(me)

    def send(src, dst, send_sem, recv_sem, partner):
        pltpu.make_async_remote_copy(
            src_ref=src, dst_ref=dst, send_sem=send_sem, recv_sem=recv_sem,
            device_id={"section": sec, "blk": partner}, device_id_type=MESH,
        ).start()

    def await_bytes(ref, sem):
        pltpu.make_async_copy(ref, ref, sem).wait()

    loads[0].wait()
    pl.semaphore_wait(barrier, expected)

    @pl.when(sec == half)
    def _():
        def call(r, c):
            signal(go, r, relay_blk(0))
            return c

        lax.fori_loop(0, half - 1, call, 0)
        signal(go, half - 1, me)

    @pl.when(sec == sections - 2)
    def _():
        pl.semaphore_wait(turn, 1)

    def send_v(t, partner):
        send(v_raw.at[:, lanes(partner)], values.at[mine], v_send, v_recv, partner)

    def send_k(t, partner):
        send(k_unit.at[:, lanes(partner)], keys.at[mine], k_send, k_recv, partner)

    def send_q(t, partner):
        send(q_unit.at[:, lanes(partner)], queries.at[token_rows(t)], q_send, q_recv.at[t // GROUP], partner)

    def own(src, dst, sem):
        pltpu.make_async_copy(src, dst, sem).start()

    each_partner(send_v, odd * (n // inner // 2))
    loads[1].wait()
    loads[5].wait()
    unit(k_raw, k_gain, k_unit)
    each_partner(send_k, odd * (n // inner // 2))
    loads[2].wait()
    loads[6].wait()
    unit(q_raw, q_gain, q_unit)
    others = pl.ds(0, (n - 1) * rows)
    if QWAIT > 0:
        await_bytes(values.at[others], v_send)
    if QWAIT > 1:
        await_bytes(values.at[others], k_send)
    each_partner(send_q)
    own(v_raw.at[:, lanes(me)], values.at[mine], v_recv)
    own(k_unit.at[:, lanes(me)], keys.at[mine], k_recv)
    own(q_unit.at[:, lanes(me)], queries.at[pl.ds(0, rows)], q_recv.at[0])

    place = lax.broadcasted_iota(jnp.int32, (1, n * rows), 1)
    loads[7].wait()
    bias = jnp.where(place < length_ref[0], 0.0, -1e30)
    scale = math.log2(math.e) / math.sqrt(HEAD)
    @pl.when(sec == sections - 1)
    def _():
        if QWAIT < 1:
            await_bytes(values.at[others], v_send)
        if QWAIT < 2:
            await_bytes(values.at[others], k_send)
        await_bytes(values.at[others], q_send)
        signal(turn, before, me)

    def slab_base(g):
        return flipped(me, low_group, bits - low_group, g)

    def slab_of(g):
        return pl.ds(pl.multiple_of(slab_base(g) // GROUP * span, span), span)

    def pass_copy(slab, g, section):
        return pltpu.make_async_remote_copy(
            src_ref=layer_out.at[:, slab], dst_ref=pass_hbm.at[0, :, slab],
            send_sem=pass_send.at[g], recv_sem=pass_recv.at[g],
            device_id={"section": section, "blk": me}, device_id_type=MESH,
        )

    def hop_copy(slab, g, buf, lane, blk):
        return pltpu.make_async_remote_copy(
            src_ref=layer_out.at[:, slab], dst_ref=buf,
            send_sem=pass_send.at[g], recv_sem=hop_recv.at[lane],
            device_id={"section": part * half + g, "blk": blk}, device_id_type=MESH,
        )

    def hand_on(buf, lane, blk):
        await_bytes(buf, hop_recv.at[lane])
        slab = pl.ds(pl.multiple_of(xor(blk // GROUP, route, groups.bit_length() - 1) * span, span), span)
        pltpu.make_async_remote_copy(
            src_ref=buf, dst_ref=pass_hbm.at[0, :, slab],
            send_sem=hop_send.at[lane], recv_sem=pass_recv.at[route],
            device_id={"section": goal, "blk": blk}, device_id_type=MESH,
        ).start()

    def hand_all_on():
        @pl.when(near)
        def _():
            hand_on(hop_near, 0, me)

        @pl.when(beside)
        def _():
            hand_on(hop_side, 1, me + 1)

    @pl.when((part == 1) & (route < half - 1))
    def _():
        hand_all_on()

    await_bytes(values, v_recv)
    await_bytes(keys, k_recv)

    def attend(g):
        here = pl.ds(pl.multiple_of(g * GROUP * rows, GROUP * rows), GROUP * rows)
        scores = lax.dot_general(
            queries[here], keys[...], (((1,), (1,)), ((), ())), preferred_element_type=jnp.float32
        )
        scores = scores * scale + bias
        weights = jnp.exp2(scores - jnp.max(scores, axis=-1, keepdims=True))
        total = jnp.sum(weights, axis=-1, keepdims=True)
        product = jnp.dot(weights.astype(jnp.bfloat16), values[...], preferred_element_type=jnp.float32)
        mixed[here] = (product / total).astype(jnp.bfloat16)

    def give_back(g):
        base = slab_base(g)
        place = attention.at[:, lanes(me)]
        for k in range(GROUP):
            out = mixed.at[token_rows(g * GROUP + k)]
            if k == 0:

                @pl.when(g > 0)
                def _(out=out):
                    send(out, place, o_send, o_recv.at[g], base)

                @pl.when(g == 0)
                def _(out=out):
                    own(out, place, o_recv.at[0])
            else:
                send(out, place, o_send, o_recv.at[g], partner_in(base, k))

    loads[3].wait()
    loads[4].wait()
    loads[8].wait()
    step = step_ref[0]

    def own_copy(slab, g):
        return pltpu.make_async_copy(layer_out.at[:, slab], out_hbm.at[0, :, slab], out_sem.at[g])

    def finish(g):
        await_bytes(mixed.at[pl.ds(0, GROUP * rows)], o_recv.at[g])
        slab = slab_of(g)
        gate = table[pl.ds(step, 1), slab]
        mix = attention[:, slab].astype(jnp.float32)
        layer_out[:, slab] = (acts[:, slab].astype(jnp.float32) + gate * mix).astype(jnp.bfloat16)
        direct = (route < half - 1) | (g == half - 1)

        @pl.when(direct)
        def _():
            pass_copy(slab, g, after).start()

        indirect = jnp.logical_not(direct)
        aside = turned(spot, part)

        @pl.when(indirect & jnp.logical_not(aside))
        def _():
            hop_copy(slab, g, hop_near, 0, me).start()

        @pl.when(indirect & aside)
        def _():
            hop_copy(slab, g, hop_side, 1, me - 1).start()

        own_copy(slab, g).start()

    def next_group(g):
        await_bytes(queries.at[pl.ds(0, GROUP * rows)], q_recv.at[g])
        attend(g)
        give_back(g)

    lag = jnp.where(far, min(LAG, groups), min(WAIT, groups))

    def early(p, c):
        next_group(p)
        return c

    def hand_on_after(g):
        @pl.when((part == 0) & (route < half - 1) & (g == jnp.minimum(route + DEFER, groups - 1)))
        def _():
            hand_all_on()

    def both(p, c):
        next_group(p)
        finish(p - lag)
        hand_on_after(p - lag)
        return c

    def late(p, c):
        finish(p)
        hand_on_after(p)
        return c

    lax.fori_loop(0, lag, early, 0)

    calls = jnp.where(far, 1, served)

    @pl.when((part == 0) & (calls > 0))
    def _():
        pl.semaphore_wait(go, calls)

    lax.fori_loop(lag, groups, both, 0)
    lax.fori_loop(groups - lag, groups, late, 0)

    @pl.when(sec < sections - 1)
    def _():
        if QWAIT < 1:
            await_bytes(values.at[others], v_send)
        if QWAIT < 2:
            await_bytes(values.at[others], k_send)
        await_bytes(values.at[others], q_send)

    await_bytes(values.at[others], o_send)

    @pl.when(helper & near)
    def _():
        await_bytes(hop_near, hop_send.at[0])

    @pl.when(helper & beside)
    def _():
        await_bytes(hop_side, hop_send.at[1])

    def settle(g, c):
        slab = slab_of(g)
        own_copy(slab, g).wait()
        pass_copy(slab, g, after).wait()
        return c

    lax.fori_loop(0, groups, settle, 0)


def body(acts, q_in, k_in, v_in, modulation, q_gain, k_gain, patch_len, timestep):
    n = lax.axis_size("blk")
    sections = lax.axis_size("section")
    _, rows, channels = acts.shape
    groups = n // GROUP
    whole = pltpu.VMEM((rows, channels), jnp.bfloat16)
    owned = pltpu.VMEM((n * rows, HEAD), jnp.bfloat16)
    out = jax.ShapeDtypeStruct(acts.shape, jnp.bfloat16)
    dma = pltpu.SemaphoreType.DMA
    kept, sent = pl.pallas_call(
        functools.partial(kernel, n, sections),
        out_shape=(out, out),
        in_specs=[pl.BlockSpec(memory_space=pltpu.MemorySpace.HBM)] * 9,
        out_specs=[pl.BlockSpec(memory_space=pl.ANY)] * 2,
        scratch_shapes=[
            whole, whole, whole, whole,
            pltpu.VMEM(modulation.shape[1:], jnp.float32),
            pltpu.VMEM((1, channels), jnp.float32),
            pltpu.VMEM((1, channels), jnp.float32),
            pltpu.SMEM((1,), jnp.int32),
            pltpu.SMEM((1,), jnp.int32),
            whole, whole, owned, owned, owned, owned, whole, whole,
            dma((9,)), dma, dma, dma, dma, dma, dma,
            dma((groups,)), dma((groups,)), dma((groups,)), dma((groups,)), dma((groups,)),
            pltpu.VMEM((rows, GROUP * HEAD), jnp.bfloat16),
            pltpu.VMEM((rows, GROUP * HEAD), jnp.bfloat16),
            dma((2,)), dma((2,)),
            pltpu.SemaphoreType.REGULAR, pltpu.SemaphoreType.REGULAR,
        ],
        compiler_params=pltpu.CompilerParams(
            collective_id=0, has_side_effects=True, vmem_limit_bytes=60 << 20
        ),
        name="relay_attention",
    )(acts, q_in, k_in, v_in, modulation, q_gain, k_gain, patch_len, timestep)

    def place(kept_in, sent_in, kept_out, sent_out, kept_buf, sent_buf, sems):
        reads = [
            pltpu.make_async_copy(kept_in, kept_buf, sems.at[0]),
            pltpu.make_async_copy(sent_in, sent_buf, sems.at[1]),
        ]
        writes = [
            pltpu.make_async_copy(kept_buf, kept_out, sems.at[2]),
            pltpu.make_async_copy(sent_buf, sent_out, sems.at[3]),
        ]
        for copy in reads:
            copy.start()
        for read, write in zip(reads, writes):
            read.wait()
            write.start()
        for copy in writes:
            copy.wait()

    return pl.pallas_call(
        place,
        out_shape=(out, out),
        in_specs=[pl.BlockSpec(memory_space=pl.ANY)] * 2,
        out_specs=[pl.BlockSpec(memory_space=pl.ANY)] * 2,
        scratch_shapes=[pltpu.VMEM(acts.shape, jnp.bfloat16)] * 2 + [dma((4,))],
        compiler_params=pltpu.CompilerParams(vmem_limit_bytes=60 << 20),
        name="place",
    )(kept, sent)


def solution(mesh):
    return jax.shard_map(
        body,
        mesh=mesh,
        in_specs=(
            P("section", "blk", None),
            P("section", "blk", None),
            P("section", "blk", None),
            P("section", "blk", None),
            P("section", None, None),
            P("section", None),
            P("section", None),
            P("section"),
            P(),
        ),
        out_specs=(P("section", "blk", None), P("section", "blk", None)),
        check_vma=False,
    )
```
